256 devices in a mesh: row: 16 (over y, x_hi, core), col: 16 (over z, x_lo).
Axes of the slice: x: 4 (x_hi: 2, x_lo: 2; x = x_hi * 2 + x_lo), y: 4, z: 8, core: 2. Of those that a mesh axis runs over, the one named last changes fastest.
Arguments:
- cell_batch: bfloat16 [2048, 20480], P('col', 'row'), may hold values from -6 to 6
- cov_prior: bfloat16 [20480, 20480], P('row', 'col'), as said below
- omega_prior: bfloat16 [20480, 20480], P('row', 'col'), as said below
Outputs:
- cov_updated: bfloat16 [20480, 20480], P('row', 'col')
- omega_panel: bfloat16 [1024, 20480], P('col', 'row')
- column_objective: float32 [1024], P('col')
The draws below stay inside these ranges and needn't reach their ends.
Inputs may be any that keep to these rules, and one draw needn't show every extreme that they name: `cov_prior`: Symmetric; its diagonal entries lie between 0.5 and 1.5. `omega_prior`: Symmetric; its diagonal entries lie between 1 and 4.
All inputs are finite; a program needn't handle non-finite values.
Results may differ from the reference program's by a relative error of at most 0.0047.
Values may be sent and summed in bfloat16 or wider, within the bound.
A program may use at most 128 MiB of HBM per device.

```python
import jax
import jax.numpy as jnp
from jax import lax

P_SIZE = 20480
PW = 64
BATCH = 2048
PANEL = 1024
N_ROW = 16


def symmetric_noise(noise_key):
    raw_values = jax.random.truncated_normal(noise_key, -4.0, 4.0, (P_SIZE, P_SIZE), jnp.float32)
    return raw_values + raw_values.T


def on_diagonal():
    return lax.iota(jnp.int32, P_SIZE)[:, None] == lax.iota(jnp.int32, P_SIZE)[None, :]


def draw_cov_prior(key, part):
    noise_key = jax.random.fold_in(key, 11)
    diag_key = jax.random.fold_in(key, 12)
    offdiag = symmetric_noise(noise_key) * 0.02
    diag_vals = jax.random.uniform(diag_key, (P_SIZE,), jnp.float32, 0.5, 1.5)
    return jnp.where(on_diagonal(), diag_vals[:, None], offdiag).astype(jnp.bfloat16)


def draw_omega_prior(key, part):
    noise_key = jax.random.fold_in(key, 21)
    scale_key = jax.random.fold_in(key, 22)
    diag_key = jax.random.fold_in(key, 23)
    positions = lax.iota(jnp.float32, P_SIZE) / P_SIZE
    roughness = jnp.exp(jax.random.uniform(scale_key, (P_SIZE,), jnp.float32, -0.3, 0.3))
    scales = 0.55 * jnp.power(3.0, positions) * roughness
    amplitude = 0.2
    outer_scale = scales[:, None] * scales[None, :]
    offdiag = symmetric_noise(noise_key) * (amplitude * outer_scale)
    diag_vals = jnp.exp(jax.random.uniform(diag_key, (P_SIZE,), jnp.float32, 0.0, 1.3862943))
    return jnp.where(on_diagonal(), diag_vals[:, None], offdiag).astype(jnp.bfloat16)


def steps_of(rng, extent, split, smallest, largest):
    def one(position, parts):
        heights = jax.random.uniform(jax.random.fold_in(jax.random.fold_in(rng, 6), position), (parts,), jnp.float32, smallest / len(split), largest / len(split))
        return jnp.repeat(jnp.exp(heights), extent[position] // parts).reshape((-1,) + (1,) * (len(extent) - position - 1))

    gain = one(*split[0])
    for cut in split[1:]:
        gain = gain * one(*cut)
    return gain


def noise(rng, shape, spread, most, pieces=(), kind=jnp.bfloat16):
    drawn = jax.random.normal(rng, shape, jnp.float32) * spread
    if len(pieces) > 0:
        drawn = steps_of(rng, shape, pieces, -0.22, 0.18) * drawn
    return jnp.clip(drawn, min=-most, max=most).astype(kind)


def setup_inputs(seed: int = 0) -> dict:
    arg_keys = jax.random.split(jax.random.key(seed), 4)
    cell_batch = noise(arg_keys[0], (BATCH, P_SIZE), 1.0, 6.0, ((0, 16), (1, 16)))
    cov_prior = draw_cov_prior(jax.random.fold_in(arg_keys[3], 71), 0)
    omega_prior = draw_omega_prior(jax.random.fold_in(arg_keys[3], 71), 0)
    return {"cell_batch": cell_batch, "cov_prior": cov_prior, "omega_prior": omega_prior}


decay_weight = 0.5
step_size = 0.2
penalty = 1.0


def panel_genes():
    row_width = P_SIZE // N_ROW
    starts = jnp.arange(N_ROW, dtype=jnp.int32)[:, None] * row_width
    return (starts + jnp.arange(PW, dtype=jnp.int32)[None, :]).reshape(-1)


def reference(cell_batch, cov_prior, omega_prior):
    row_width = P_SIZE // N_ROW
    scale_new = (1.0 - decay_weight) / BATCH
    numbers = jnp.arange(N_ROW, dtype=jnp.int32)

    def cov_rows_of(number):
        offset = number * row_width
        genes_slab = lax.dynamic_slice_in_dim(cell_batch, offset, row_width, 1)
        product = lax.dot_general(genes_slab, cell_batch, (((0,), (0,)), ((), ())), preferred_element_type=jnp.float32)
        prior_rows = lax.dynamic_slice_in_dim(cov_prior, offset, row_width, 0).astype(jnp.float32)
        return (decay_weight * prior_rows + scale_new * product).astype(jnp.bfloat16)

    cov_updated = lax.map(cov_rows_of, numbers).reshape(P_SIZE, P_SIZE)
    genes = panel_genes()
    cov_rows = cov_updated[genes]
    omega_rows = omega_prior[genes]

    def panel_part(number):
        offset = number * row_width
        omega_part = lax.dynamic_slice_in_dim(omega_prior, offset, row_width, 0)
        cov_part = lax.dynamic_slice_in_dim(cov_updated, offset, row_width, 0)
        first_term = lax.dot_general(cov_rows, omega_part, (((1,), (1,)), ((), ())), preferred_element_type=jnp.float32)
        second_term = lax.dot_general(omega_rows, cov_part, (((1,), (1,)), ((), ())), preferred_element_type=jnp.float32)
        return first_term, second_term

    first_all, second_all = lax.map(panel_part, numbers)
    first_all = jnp.transpose(first_all, (1, 0, 2)).reshape(PANEL, P_SIZE)
    second_all = jnp.transpose(second_all, (1, 0, 2)).reshape(PANEL, P_SIZE)
    omega_vals = omega_rows.astype(jnp.float32)
    diagonal = genes[:, None] == jnp.arange(P_SIZE, dtype=jnp.int32)[None, :]
    own_diag = jnp.sum(jnp.where(diagonal, omega_vals, jnp.float32(0.0)), axis=1)
    inverse = jnp.where(diagonal, 1.0 / own_diag[:, None], jnp.float32(0.0))
    gradient = 0.5 * (first_all + second_all) - inverse
    stepped = omega_vals - step_size * gradient
    shrunk = jnp.sign(stepped) * jnp.maximum(jnp.abs(stepped) - step_size * penalty, 0.0)
    omega_panel = jnp.where(diagonal, stepped, shrunk).astype(jnp.bfloat16)
    quadratic = 0.5 * jnp.sum(omega_vals * second_all, axis=1)
    lasso = penalty * jnp.sum(jnp.where(diagonal, jnp.float32(0.0), jnp.abs(omega_vals)), axis=1)
    column_objective = (quadratic + lasso - jnp.log(own_diag)) / P_SIZE
    return cov_updated, omega_panel, column_objective
```

```python
import functools

import jax
import jax.numpy as jnp
from jax import lax
from jax.experimental import pallas as pl
from jax.experimental.pallas import tpu as pltpu
from jax.sharding import PartitionSpec as P

P_SIZE = 20480
PW = 64

decay_weight = 0.5
step_size = 0.2
penalty = 1.0

MESH = pl.DeviceIdType.MESH
N_SEM = 192
XROWS = 64


def rows(ref, start, size, unit=16):
    if isinstance(start, int):
        return ref.at[pl.ds(start, size), :]
    return ref.at[pl.ds(pl.multiple_of(start, unit), size), :]


def nt(a, b):
    return lax.dot_general(a, b, (((1,), (1,)), ((), ())), preferred_element_type=jnp.float32)


def kernel(
    x_hbm, s_hbm, om_hbm, cov_hbm, panel_ref, obj_ref,
    xr, xc, po, pc, om, cv, acc, p1, ov, st2, rv2, st1, rv1, tot, oslots, tr,
    send_sem, recv_sem, load_sem,
):
    r = lax.axis_index("row")
    c = lax.axis_index("col")
    y, xh, core = lax.div(r, 4), lax.rem(lax.div(r, 2), 2), lax.rem(r, 2)
    z, xl = lax.div(c, 2), lax.rem(c, 2)
    width = om.shape[0]
    piece = x_hbm.shape[0]

    def rowid(yy, hh, kk):
        return lax.rem(yy + 8, 4) * 4 + hh * 2 + kk

    def colid(zz, ll):
        return lax.rem(zz + 16, 8) * 2 + ll

    d_zp, d_zm = (r, colid(z + 1, xl)), (r, colid(z - 1, xl))
    d_xl = (r, colid(z, 1 - xl))
    d_yp, d_ym = (rowid(y + 1, xh, core), c), (rowid(y - 1, xh, core), c)
    d_xh = (rowid(y, 1 - xh, core), c)
    d_core = (rowid(y, xh, 1 - core), c)
    d_tr = (c, r)

    load_x = pltpu.make_async_copy(x_hbm, rows(xr, c * piece, piece), load_sem.at[0])
    load_x.start()
    load_po = pltpu.make_async_copy(om_hbm.at[pl.ds(0, PW), :], rows(po, r * PW, PW), load_sem.at[1])
    load_po.start()
    load_om = pltpu.make_async_copy(om_hbm, om, load_sem.at[2])
    load_om.start()
    load_s = pltpu.make_async_copy(s_hbm, cv, load_sem.at[3])
    load_s.start()

    barrier = pltpu.get_barrier_semaphore()

    def greet(dev):
        pl.semaphore_signal(barrier, inc=1, device_id=dev, device_id_type=MESH)

    for i in range(1, 16):
        greet((lax.rem(r + i, 16), c))
    for dev in (d_zp, d_zm, d_xl):
        greet(dev)

    @pl.when(r != c)
    def _():
        greet(d_tr)
        pl.semaphore_wait(barrier, 19)

    @pl.when(r == c)
    def _():
        pl.semaphore_wait(barrier, 18)

    started = []
    count = [0]

    def new(n=1):
        first = count[0]
        count[0] += n
        assert count[0] <= N_SEM
        return first

    def desc(i, src, dst, dev):
        return pltpu.make_async_remote_copy(
            src_ref=src, dst_ref=dst, send_sem=send_sem.at[i], recv_sem=recv_sem.at[i],
            device_id=dev, device_id_type=MESH,
        )

    def send(i, src, dst, dev):
        d = desc(i, src, dst, dev)
        d.start()
        started.append(d)

    def arrived(i, slot):
        desc(i, slot, slot, d_core).wait_recv()

    class RowGather:
        def __init__(self, buf, m):
            self.buf, self.m, self.b = buf, m, new(19)
            self.h = m // 2

        def slot(self, yy, hh, kk, lo=0, n=None):
            return rows(self.buf, rowid(yy, hh, kk) * self.m + lo, n or self.m)

        def go(self, i, dev, yy, hh, lo=0, n=None):
            s = self.slot(yy, hh, core, lo, n)
            send(self.b + i, s, s, dev)

        def wait(self, i, yy, hh, lo=0, n=None, kk=None):
            arrived(self.b + i, self.slot(yy, hh, core if kk is None else kk, lo, n))

        def s0(self):
            self.go(0, d_xh, y, xh)
            self.go(1, d_yp, y, xh)
            self.go(2, d_ym, y, xh)
            self.go(9, d_core, y, xh)

        def s1(self):
            o = 1 - xh
            self.wait(0, y, o)
            self.go(3, d_yp, y, o)
            self.go(4, d_ym, y, o)
            self.go(10, d_core, y, o)

        def s2(self):
            h = self.h
            self.wait(1, y - 1, xh)
            self.go(5, d_yp, y - 1, xh, h, h)
            self.wait(2, y + 1, xh)
            self.go(6, d_ym, y + 1, xh, 0, h)
            self.go(11, d_core, y - 1, xh)
            self.go(12, d_core, y + 1, xh)

        def s3(self):
            h, o = self.h, 1 - xh
            self.wait(3, y - 1, o)
            self.go(7, d_yp, y - 1, o, h, h)
            self.wait(4, y + 1, o)
            self.go(8, d_ym, y + 1, o, 0, h)
            self.go(13, d_core, y - 1, o)
            self.go(14, d_core, y + 1, o)

        def s4(self):
            h, o = self.h, 1 - xh
            self.wait(5, y + 2, xh, h, h)
            self.go(15, d_core, y + 2, xh, h, h)
            self.wait(6, y + 2, xh, 0, h)
            self.go(16, d_core, y + 2, xh, 0, h)
            self.wait(7, y + 2, o, h, h)
            self.go(17, d_core, y + 2, o, h, h)
            self.wait(8, y + 2, o, 0, h)
            self.go(18, d_core, y + 2, o, 0, h)

        def s5(self):
            h, o, k = self.h, 1 - xh, 1 - core
            self.wait(9, y, xh, kk=k)
            self.wait(10, y, o, kk=k)
            self.wait(11, y - 1, xh, kk=k)
            self.wait(12, y + 1, xh, kk=k)
            self.wait(13, y - 1, o, kk=k)
            self.wait(14, y + 1, o, kk=k)
            self.wait(15, y + 2, xh, h, h, kk=k)
            self.wait(16, y + 2, xh, 0, h, kk=k)
            self.wait(17, y + 2, o, h, h, kk=k)
            self.wait(18, y + 2, o, 0, h, kk=k)

    g, gh = XROWS, XROWS // 2
    ph = piece // 2
    cg = {}

    def cid(*key):
        if key not in cg:
            cg[key] = new()
        return cg[key]

    def xs(zz, ll, lo=0, n=piece):
        return rows(xr, colid(zz, ll) * piece + lo, n)

    def csend(key, dev, zz, ll, lo=0, n=piece):
        s = xs(zz, ll, lo, n)
        send(cid(*key), s, s, dev)

    def cwait(key, zz, ll, lo=0, n=piece):
        arrived(cid(*key), xs(zz, ll, lo, n))

    rest = piece - g

    def col0():
        csend(("a",), d_xl, z, xl, 0, g)
        csend(("p+", 1), d_zp, z, xl)
        csend(("p-", 1), d_zm, z, xl)
        csend(("f", 0), d_xl, z, xl, g, rest)

    def col1():
        cwait(("a",), z, 1 - xl, 0, g)
        csend(("q+", 1), d_zp, z, 1 - xl, 0, g)
        csend(("q-", 1), d_zm, z, 1 - xl, 0, g)

    def colp(d):
        cwait(("p+", d), z - d, xl)
        if d < 3:
            csend(("p+", d + 1), d_zp, z - d, xl)
        else:
            csend(("p+", 4), d_zp, z - d, xl, 0, ph)
        csend(("f+", d), d_xl, z - d, xl, g, rest)
        cwait(("p-", d), z + d, xl)
        if d < 3:
            csend(("p-", d + 1), d_zm, z + d, xl)
        else:
            csend(("p-", 4), d_zm, z + d, xl, ph, ph)
        csend(("f-", d), d_xl, z + d, xl, g, rest)

    def colq(d):
        cwait(("q+", d), z - d, 1 - xl, 0, g)
        if d < 3:
            csend(("q+", d + 1), d_zp, z - d, 1 - xl, 0, g)
        else:
            csend(("q+", 4), d_zp, z - d, 1 - xl, 0, gh)
        cwait(("q-", d), z + d, 1 - xl, 0, g)
        if d < 3:
            csend(("q-", d + 1), d_zm, z + d, 1 - xl, 0, g)
        else:
            csend(("q-", 4), d_zm, z + d, 1 - xl, gh, gh)

    def colp4():
        cwait(("p-", 4), z + 4, xl, ph, ph)
        csend(("f", 4), d_xl, z + 4, xl, ph, ph)
        cwait(("p+", 4), z + 4, xl, 0, ph)

    def colq4():
        cwait(("q+", 4), z + 4, 1 - xl, 0, gh)
        cwait(("q-", 4), z + 4, 1 - xl, gh, gh)

    def colf(d):
        if d == 0:
            cwait(("f", 0), z, 1 - xl, g, rest)
        elif d == 4:
            cwait(("f", 4), z + 4, 1 - xl, ph, ph)
        else:
            cwait(("f+", d), z - d, 1 - xl, g, rest)
            cwait(("f-", d), z + d, 1 - xl, g, rest)

    assert g == ph

    gx = RowGather(xc, piece)
    go_ = RowGather(po, PW)
    tid = new()
    load_x.wait()
    own_x = rows(xr, c * piece, piece)

    @pl.when(r != c)
    def _():
        desc(tid, own_x, rows(xc, c * piece, piece), d_tr).start()

    @pl.when(r == c)
    def _():
        pltpu.make_async_copy(own_x, rows(xc, c * piece, piece), load_sem.at[4]).start()

    col0()
    load_po.wait()
    go_.s0()
    acc[...] = jnp.zeros_like(acc)
    col1()

    @pl.when(r != c)
    def _():
        desc(tid, own_x, rows(xc, r * piece, piece), d_tr).wait_recv()

    @pl.when(r == c)
    def _():
        pltpu.make_async_copy(own_x, rows(xc, r * piece, piece), load_sem.at[4]).wait()

    gx.s0()
    go_.s1()
    gx.s1()
    colp(1)
    go_.s2()
    colq(1)
    go_.s3()
    gx.s2()
    colp(2)
    go_.s4()
    colq(2)
    gx.s3()
    load_om.wait()
    turned = jnp.transpose(om[:, :128].astype(jnp.float32))
    ov[...] = turned[:PW, :]
    colp(3)
    gx.s4()
    colq(3)
    gx.s5()

    tile = 256

    def accumulate(lo, n):
        def body(i, carry):
            j = lax.rem(z + lo + i + 8, 8)
            k0 = pl.multiple_of(j * 2 * piece, 2 * piece)

            def inner(m, carry2):
                m0 = pl.multiple_of(m * tile, tile)
                a = xr[pl.ds(k0, 2 * piece), pl.ds(m0, tile)]
                b = xc[pl.ds(k0, 2 * piece), :]
                acc[pl.ds(m0, tile), :] += lax.dot_general(
                    a, b, (((0,), (0,)), ((), ())), preferred_element_type=jnp.float32
                )
                return carry2

            return lax.fori_loop(0, width // tile, inner, carry)

        lax.fori_loop(0, n, body, 0)

    colf(0)
    colf(1)
    colf(2)
    accumulate(-2, 5)
    colp4()
    colf(3)
    accumulate(3, 1)
    accumulate(-3, 1)
    colq4()
    colf(4)
    accumulate(4, 1)
    go_.s5()

    scale_new = (1.0 - decay_weight) / 2048
    load_s.wait()

    def finalize(lo, n):
        lo = lo if isinstance(lo, int) else pl.multiple_of(lo, 128)
        prior = cv[pl.ds(lo, n), :].astype(jnp.float32)
        cv[pl.ds(lo, n), :] = (decay_weight * prior + scale_new * acc[pl.ds(lo, n), :]).astype(jnp.bfloat16)

    finalize(0, 128)
    own_cov = pltpu.make_async_copy(cv.at[pl.ds(0, PW), :], rows(pc, r * PW, PW), load_sem.at[5])

    def fin_body(i, carry):
        finalize(128 + i * 128, 128)
        return carry

    lax.fori_loop(0, 2, fin_body, 0)
    own_cov.start()
    own_cov.wait()
    gc = RowGather(pc, PW)
    gc.s0()
    lax.fori_loop(2, width // 128 - 1, fin_body, 0)

    def product(dst, left, right):
        def body(m, carry):
            m0 = pl.multiple_of(m * tile, tile)
            dst[pl.ds(m0, tile), :] = nt(left[pl.ds(m0, tile), :], right[...])
            return carry

        lax.fori_loop(0, 16 * PW // tile, body, 0)

    class Scatter:
        def __init__(self, src, st, rv):
            self.src, self.st, self.rv = src, st, rv
            self.ids = {}
            for n, key in enumerate(
                [("+", 0, 0), ("-", 0, 1)]
                + [(d, s, h) for s in (1, 2, 3) for d in "+-" for h in (0, 1)]
                + [("x", 0, 0)]
            ):
                self.ids[key] = (n, new())

        def own(self, zz, h):
            return self.src[pl.ds(pl.multiple_of(colid(zz, h) * PW, PW), PW), :]

        def slot(self, buf, key):
            n = self.ids[key][0]
            return buf.at[pl.ds(n * PW, PW), :]

        def got(self, key):
            s = self.slot(self.rv, key)
            arrived(self.ids[key][1], s)
            return s[...].astype(jnp.float32)

        def put(self, key, value, dev):
            s = self.slot(self.st, key)
            s[...] = value.astype(jnp.bfloat16)
            send(self.ids[key][1], s, self.slot(self.rv, key), dev)

        def step(self, s):
            for d, h in ((("+"), 0), ("-", 1), ("-", 0), ("+", 1)):
                key = (d, s, h)
                if key not in self.ids:
                    continue
                zz = z + 4 - s if d == "+" else z - 4 + s
                value = self.own(zz, h)
                if (d, s - 1, h) in self.ids:
                    value = value + self.got((d, s - 1, h))
                self.put(key, value, d_zp if d == "+" else d_zm)

        def close(self):
            for h in (0, 1):
                tot[h * PW:(h + 1) * PW, :] = (
                    self.own(z, h) + self.got(("+", 3, h)) + self.got(("-", 3, h))
                )
            self.put(("x", 0, 0), tot[pl.ds(pl.multiple_of((1 - xl) * PW, PW), PW), :], d_xl)

        def result(self):
            return tot[pl.ds(pl.multiple_of(xl * PW, PW), PW), :] + self.got(("x", 0, 0))

    product(acc, po, cv)
    store_cov = pltpu.make_async_copy(cv, cov_hbm, load_sem.at[6])
    store_cov.start()
    rs2 = Scatter(acc, st2, rv2)
    rs1 = Scatter(p1, st1, rv1)
    rs2.step(0)
    gc.s1()
    rs2.step(1)
    gc.s2()
    rs2.step(2)
    gc.s3()
    rs2.step(3)
    gc.s4()
    rs2.close()
    gc.s5()

    product(p1, pc, om)
    second_sum = rs2.result()
    acc[0:PW, :] = second_sum
    rs1.step(0)
    rs1.step(1)

    omega_vals = ov[...]
    lane = lax.broadcasted_iota(jnp.int32, (PW, width), 1)
    sub = lax.broadcasted_iota(jnp.int32, (PW, width), 0)
    diagonal = (lane == sub) & (r == c)
    own_diag = jnp.where(diagonal, omega_vals, 1.0)
    terms = 0.5 * omega_vals * acc[0:PW, :] + jnp.where(
        diagonal, -jnp.log(own_diag), penalty * jnp.abs(omega_vals)
    )
    tr[...] = jnp.zeros_like(tr)
    part = terms[:, 0:128]
    for t in range(1, width // 128):
        part = part + terms[:, t * 128:(t + 1) * 128]
    tr[0:PW, :] = part
    line = jnp.sum(jnp.transpose(tr[...]), axis=0, keepdims=True)
    oslots[pl.ds(pl.multiple_of(r * 8, 8), 8), :] = jnp.broadcast_to(line, (8, 128))
    oid = new(16)

    rs1.step(2)
    mine = rows(oslots, r * 8, 8, 8)
    for i in range(1, 16):
        send(oid + i, mine, mine, (lax.rem(r + i, 16), c))
    rs1.step(3)
    rs1.close()
    for i in range(1, 16):
        arrived(oid + i, rows(oslots, lax.rem(r + 16 - i, 16) * 8, 8, 8))
    total = oslots[0:8, :]
    for i in range(1, 16):
        total = total + oslots[i * 8:(i + 1) * 8, :]
    obj_ref[...] = total / P_SIZE

    both = rs1.result() + acc[0:PW, :]
    gradient = 0.5 * both - jnp.where(diagonal, 1.0 / own_diag, 0.0)
    stepped = omega_vals - step_size * gradient
    limit = step_size * penalty
    shrunk = stepped - jnp.clip(stepped, -limit, limit)
    panel_ref[...] = jnp.where(diagonal, stepped, shrunk).astype(jnp.bfloat16)

    store_cov.wait()
    for d in started:
        d.wait_send()

    @pl.when(r != c)
    def _():
        desc(tid, own_x, rows(xc, r * piece, piece), d_tr).wait_send()


def per_device(cell_batch, cov_prior, omega_prior):
    piece, width = cell_batch.shape
    any_ = pl.BlockSpec(memory_space=pl.ANY)
    vmem = pl.BlockSpec(memory_space=pltpu.VMEM)
    bf, f32 = jnp.bfloat16, jnp.float32
    cov, panel, obj = pl.pallas_call(
        kernel,
        out_shape=(
            jax.ShapeDtypeStruct((width, width), bf),
            jax.ShapeDtypeStruct((PW, width), bf),
            jax.ShapeDtypeStruct((8, 128), f32),
        ),
        in_specs=[any_] * 3,
        out_specs=(any_, vmem, vmem),
        scratch_shapes=[
            pltpu.VMEM((16 * piece, width), bf),
            pltpu.VMEM((16 * piece, width), bf),
            pltpu.VMEM((16 * PW, width), bf),
            pltpu.VMEM((16 * PW, width), bf),
            pltpu.VMEM((width, width), bf),
            pltpu.VMEM((width, width), bf),
            pltpu.VMEM((width, width), f32),
            pltpu.VMEM((16 * PW, width), f32),
            pltpu.VMEM((PW, width), f32),
            pltpu.VMEM((15 * PW, width), bf),
            pltpu.VMEM((15 * PW, width), bf),
            pltpu.VMEM((15 * PW, width), bf),
            pltpu.VMEM((15 * PW, width), bf),
            pltpu.VMEM((2 * PW, width), f32),
            pltpu.VMEM((128, 128), f32),
            pltpu.VMEM((128, 128), f32),
            pltpu.SemaphoreType.DMA((N_SEM,)),
            pltpu.SemaphoreType.DMA((N_SEM,)),
            pltpu.SemaphoreType.DMA((8,)),
        ],
        compiler_params=pltpu.CompilerParams(
            collective_id=0, has_side_effects=True, vmem_limit_bytes=62 * 1024 * 1024
        ),
    )(cell_batch, cov_prior, omega_prior)
    return cov, panel, obj[0, :PW]


def solution(mesh):
    return jax.shard_map(
        per_device,
        mesh=mesh,
        in_specs=(P("col", "row"), P("row", "col"), P("row", "col")),
        out_specs=(P("row", "col"), P("col", "row"), P("col")),
        check_vma=False,
    )
```

```python
import functools

import jax
import jax.numpy as jnp
from jax import lax
from jax.experimental import pallas as pl
from jax.experimental.pallas import tpu as pltpu
from jax.sharding import PartitionSpec as P

P_SIZE = 20480
PW = 64

decay_weight = 0.5
step_size = 0.2
penalty = 1.0

MESH = pl.DeviceIdType.MESH
N_SEM = 192
XROWS = 64


def rows(ref, start, size, unit=16):
    if isinstance(start, int):
        return ref.at[pl.ds(start, size), :]
    return ref.at[pl.ds(pl.multiple_of(start, unit), size), :]


def nt(a, b):
    return lax.dot_general(a, b, (((1,), (1,)), ((), ())), preferred_element_type=jnp.float32)


def kernel(
    x_hbm, s_hbm, om_hbm, cov_hbm, panel_ref, obj_ref,
    xr, xc, mid, po, pc, om, cv, acc, p1, ov, st2, rv2, st1, rv1, tot, oslots, tr,
    send_sem, recv_sem, load_sem,
):
    r = lax.axis_index("row")
    c = lax.axis_index("col")
    y, xh, core = lax.div(r, 4), lax.rem(lax.div(r, 2), 2), lax.rem(r, 2)
    z, xl = lax.div(c, 2), lax.rem(c, 2)
    width = om.shape[0]
    piece = x_hbm.shape[0]

    def rowid(yy, hh, kk):
        return lax.rem(yy + 8, 4) * 4 + hh * 2 + kk

    def colid(zz, ll):
        return lax.rem(zz + 16, 8) * 2 + ll

    d_zp, d_zm = (r, colid(z + 1, xl)), (r, colid(z - 1, xl))
    d_xl = (r, colid(z, 1 - xl))
    d_yp, d_ym = (rowid(y + 1, xh, core), c), (rowid(y - 1, xh, core), c)
    d_xh = (rowid(y, 1 - xh, core), c)
    d_core = (rowid(y, xh, 1 - core), c)

    shift = lax.rem(lax.div(z + xh, 2), 4)
    d_mid = (rowid(y + shift, xh, core), c)
    from_row = rowid(y + 4 - shift, xh, core)
    to_row = lax.rem(c + from_row - core, 16)
    d_tr = (to_row, from_row)
    tr_local = (to_row == r) & (from_row == c)
    cells = lax.rem(r + 16 - 2 * z, 16)
    back = lax.rem(lax.div(lax.div(cells, 2) + lax.rem(z, 2), 2), 4)
    d_src = (rowid(lax.div(z, 2) + back, lax.rem(z, 2), xl), cells)

    load_x = pltpu.make_async_copy(x_hbm, rows(xr, c * piece, piece), load_sem.at[0])
    load_x.start()
    load_po = pltpu.make_async_copy(om_hbm.at[pl.ds(0, PW), :], rows(po, r * PW, PW), load_sem.at[1])
    load_po.start()
    load_om = pltpu.make_async_copy(om_hbm, om, load_sem.at[2])
    load_om.start()
    load_s = pltpu.make_async_copy(s_hbm, cv, load_sem.at[3])
    load_s.start()

    barrier = pltpu.get_barrier_semaphore()

    def greet(dev):
        pl.semaphore_signal(barrier, inc=1, device_id=dev, device_id_type=MESH)

    for i in range(1, 16):
        greet((lax.rem(r + i, 16), c))
    for dev in (d_zp, d_zm, d_xl):
        greet(dev)

    @pl.when(jnp.logical_not(tr_local))
    def _():
        greet(d_src)
        pl.semaphore_wait(barrier, 19)

    @pl.when(tr_local)
    def _():
        pl.semaphore_wait(barrier, 18)

    started = []
    count = [0]

    def new(n=1):
        first = count[0]
        count[0] += n
        assert count[0] <= N_SEM
        return first

    def desc(i, src, dst, dev):
        return pltpu.make_async_remote_copy(
            src_ref=src, dst_ref=dst, send_sem=send_sem.at[i], recv_sem=recv_sem.at[i],
            device_id=dev, device_id_type=MESH,
        )

    def send(i, src, dst, dev):
        d = desc(i, src, dst, dev)
        d.start()
        started.append(d)

    def arrived(i, slot):
        desc(i, slot, slot, d_core).wait_recv()

    class RowGather:
        def __init__(self, buf, m):
            self.buf, self.m, self.b = buf, m, new(19)
            self.h = m // 2

        def slot(self, yy, hh, kk, lo=0, n=None):
            return rows(self.buf, rowid(yy, hh, kk) * self.m + lo, n or self.m)

        def go(self, i, dev, yy, hh, lo=0, n=None):
            s = self.slot(yy, hh, core, lo, n)
            send(self.b + i, s, s, dev)

        def wait(self, i, yy, hh, lo=0, n=None, kk=None):
            arrived(self.b + i, self.slot(yy, hh, core if kk is None else kk, lo, n))

        def s0(self):
            self.go(0, d_xh, y, xh)
            self.go(1, d_yp, y, xh)
            self.go(2, d_ym, y, xh)
            self.go(9, d_core, y, xh)

        def s1(self):
            o = 1 - xh
            self.wait(0, y, o)
            self.go(3, d_yp, y, o)
            self.go(4, d_ym, y, o)
            self.go(10, d_core, y, o)

        def s2(self):
            h = self.h
            self.wait(1, y - 1, xh)
            self.go(5, d_yp, y - 1, xh, h, h)
            self.wait(2, y + 1, xh)
            self.go(6, d_ym, y + 1, xh, 0, h)
            self.go(11, d_core, y - 1, xh)
            self.go(12, d_core, y + 1, xh)

        def s3(self):
            h, o = self.h, 1 - xh
            self.wait(3, y - 1, o)
            self.go(7, d_yp, y - 1, o, h, h)
            self.wait(4, y + 1, o)
            self.go(8, d_ym, y + 1, o, 0, h)
            self.go(13, d_core, y - 1, o)
            self.go(14, d_core, y + 1, o)

        def s4(self):
            h, o = self.h, 1 - xh
            self.wait(5, y + 2, xh, h, h)
            self.go(15, d_core, y + 2, xh, h, h)
            self.wait(6, y + 2, xh, 0, h)
            self.go(16, d_core, y + 2, xh, 0, h)
            self.wait(7, y + 2, o, h, h)
            self.go(17, d_core, y + 2, o, h, h)
            self.wait(8, y + 2, o, 0, h)
            self.go(18, d_core, y + 2, o, 0, h)

        def s5(self):
            h, o, k = self.h, 1 - xh, 1 - core
            self.wait(9, y, xh, kk=k)
            self.wait(10, y, o, kk=k)
            self.wait(11, y - 1, xh, kk=k)
            self.wait(12, y + 1, xh, kk=k)
            self.wait(13, y - 1, o, kk=k)
            self.wait(14, y + 1, o, kk=k)
            self.wait(15, y + 2, xh, h, h, kk=k)
            self.wait(16, y + 2, xh, 0, h, kk=k)
            self.wait(17, y + 2, o, h, h, kk=k)
            self.wait(18, y + 2, o, 0, h, kk=k)

    g, gh = XROWS, XROWS // 2
    ph = piece // 2
    cg = {}

    def cid(*key):
        if key not in cg:
            cg[key] = new()
        return cg[key]

    def xs(zz, ll, lo=0, n=piece):
        return rows(xr, colid(zz, ll) * piece + lo, n)

    def csend(key, dev, zz, ll, lo=0, n=piece):
        s = xs(zz, ll, lo, n)
        send(cid(*key), s, s, dev)

    def cwait(key, zz, ll, lo=0, n=piece):
        arrived(cid(*key), xs(zz, ll, lo, n))

    rest = piece - g

    def col0():
        csend(("a",), d_xl, z, xl, 0, g)
        csend(("p+", 1), d_zp, z, xl)
        csend(("p-", 1), d_zm, z, xl)
        csend(("f", 0), d_xl, z, xl, g, rest)

    def col1():
        cwait(("a",), z, 1 - xl, 0, g)
        csend(("q+", 1), d_zp, z, 1 - xl, 0, g)
        csend(("q-", 1), d_zm, z, 1 - xl, 0, g)

    def colp(d):
        cwait(("p+", d), z - d, xl)
        if d < 3:
            csend(("p+", d + 1), d_zp, z - d, xl)
        else:
            csend(("p+", 4), d_zp, z - d, xl, 0, ph)
        csend(("f+", d), d_xl, z - d, xl, g, rest)
        cwait(("p-", d), z + d, xl)
        if d < 3:
            csend(("p-", d + 1), d_zm, z + d, xl)
        else:
            csend(("p-", 4), d_zm, z + d, xl, ph, ph)
        csend(("f-", d), d_xl, z + d, xl, g, rest)

    def colq(d):
        cwait(("q+", d), z - d, 1 - xl, 0, g)
        if d < 3:
            csend(("q+", d + 1), d_zp, z - d, 1 - xl, 0, g)
        else:
            csend(("q+", 4), d_zp, z - d, 1 - xl, 0, gh)
        cwait(("q-", d), z + d, 1 - xl, 0, g)
        if d < 3:
            csend(("q-", d + 1), d_zm, z + d, 1 - xl, 0, g)
        else:
            csend(("q-", 4), d_zm, z + d, 1 - xl, gh, gh)

    def colp4():
        cwait(("p-", 4), z + 4, xl, ph, ph)
        csend(("f", 4), d_xl, z + 4, xl, ph, ph)
        cwait(("p+", 4), z + 4, xl, 0, ph)

    def colq4():
        cwait(("q+", 4), z + 4, 1 - xl, 0, gh)
        cwait(("q-", 4), z + 4, 1 - xl, gh, gh)

    def colf(d):
        if d == 0:
            cwait(("f", 0), z, 1 - xl, g, rest)
        elif d == 4:
            cwait(("f", 4), z + 4, 1 - xl, ph, ph)
        else:
            cwait(("f+", d), z - d, 1 - xl, g, rest)
            cwait(("f-", d), z + d, 1 - xl, g, rest)

    assert g == ph

    gx = RowGather(xc, piece)
    go_ = RowGather(po, PW)
    tid = new(4)
    halves = (0, 1)
    load_x.wait()

    def to_mid(h):
        return desc(tid + h, rows(xr, c * piece + h * ph, ph), rows(mid, h * ph, ph), d_mid)

    def to_slot(h):
        return desc(tid + 2 + h, rows(mid, h * ph, ph), rows(xc, to_row * piece + h * ph, ph), d_tr)

    def keep():
        return pltpu.make_async_copy(rows(xr, c * piece, piece), mid, load_sem.at[4])

    def land():
        return pltpu.make_async_copy(mid, rows(xc, r * piece, piece), load_sem.at[7])

    @pl.when(shift != 0)
    def _():
        for h in halves:
            to_mid(h).start()

    @pl.when(shift == 0)
    def _():
        keep().start()

    col0()
    load_po.wait()
    go_.s0()

    @pl.when(shift == 0)
    def _():
        keep().wait()

    for h in halves:
        @pl.when(shift != 0)
        def _(h=h):
            to_mid(h).wait_recv()

        @pl.when(jnp.logical_not(tr_local))
        def _(h=h):
            to_slot(h).start()

    @pl.when(tr_local)
    def _():
        land().start()

    acc[...] = jnp.zeros_like(acc)
    col1()
    go_.s1()
    colp(1)
    colq(1)
    go_.s2()

    @pl.when(jnp.logical_not(tr_local))
    def _():
        for h in halves:
            desc(tid + 2 + h, rows(mid, h * ph, ph), rows(xc, r * piece + h * ph, ph), d_tr).wait_recv()

    @pl.when(tr_local)
    def _():
        land().wait()

    gx.s0()
    go_.s3()
    gx.s1()
    colp(2)
    gx.s2()
    go_.s4()
    colq(2)
    gx.s3()
    load_om.wait()
    turned = jnp.transpose(om[:, :128].astype(jnp.float32))
    ov[...] = turned[:PW, :]
    colp(3)
    gx.s4()
    colq(3)
    gx.s5()

    tile = 256

    def accumulate(lo, n):
        def body(i, carry):
            j = lax.rem(z + lo + i + 8, 8)
            k0 = pl.multiple_of(j * 2 * piece, 2 * piece)
            s0 = pl.multiple_of(lax.rem(j + z, 8) * 2 * piece, 2 * piece)

            def inner(m, carry2):
                m0 = pl.multiple_of(m * tile, tile)
                a = xr[pl.ds(k0, 2 * piece), pl.ds(m0, tile)]
                b = xc[pl.ds(s0, 2 * piece), :]
                acc[pl.ds(m0, tile), :] += lax.dot_general(
                    a, b, (((0,), (0,)), ((), ())), preferred_element_type=jnp.float32
                )
                return carry2

            return lax.fori_loop(0, width // tile, inner, carry)

        lax.fori_loop(0, n, body, 0)

    colf(0)
    colf(1)
    colf(2)
    accumulate(-2, 5)
    colp4()
    colf(3)
    accumulate(3, 1)
    accumulate(-3, 1)
    colq4()
    colf(4)
    accumulate(4, 1)
    go_.s5()

    scale_new = (1.0 - decay_weight) / 2048
    load_s.wait()

    def finalize(lo, n):
        lo = lo if isinstance(lo, int) else pl.multiple_of(lo, 128)
        prior = cv[pl.ds(lo, n), :].astype(jnp.float32)
        cv[pl.ds(lo, n), :] = (decay_weight * prior + scale_new * acc[pl.ds(lo, n), :]).astype(jnp.bfloat16)

    finalize(0, 128)
    own_cov = pltpu.make_async_copy(cv.at[pl.ds(0, PW), :], rows(pc, r * PW, PW), load_sem.at[5])

    def fin_body(i, carry):
        finalize(128 + i * 128, 128)
        return carry

    lax.fori_loop(0, 2, fin_body, 0)
    own_cov.start()
    own_cov.wait()
    gc = RowGather(pc, PW)
    gc.s0()
    lax.fori_loop(2, width // 128 - 1, fin_body, 0)

    def product(dst, left, right):
        def body(m, carry):
            m0 = pl.multiple_of(m * tile, tile)
            dst[pl.ds(m0, tile), :] = nt(left[pl.ds(m0, tile), :], right[...])
            return carry

        lax.fori_loop(0, 16 * PW // tile, body, 0)

    class Scatter:
        def __init__(self, src, st, rv):
            self.src, self.st, self.rv = src, st, rv
            self.ids = {}
            for n, key in enumerate(
                [("+", 0, 0), ("-", 0, 1)]
                + [(d, s, h) for s in (1, 2, 3) for d in "+-" for h in (0, 1)]
                + [("x", 0, 0)]
            ):
                self.ids[key] = (n, new())

        def own(self, zz, h):
            return self.src[pl.ds(pl.multiple_of(colid(zz, h) * PW, PW), PW), :]

        def slot(self, buf, key):
            n = self.ids[key][0]
            return buf.at[pl.ds(n * PW, PW), :]

        def got(self, key):
            s = self.slot(self.rv, key)
            arrived(self.ids[key][1], s)
            return s[...].astype(jnp.float32)

        def put(self, key, value, dev):
            s = self.slot(self.st, key)
            s[...] = value.astype(jnp.bfloat16)
            send(self.ids[key][1], s, self.slot(self.rv, key), dev)

        def step(self, s):
            for d, h in ((("+"), 0), ("-", 1), ("-", 0), ("+", 1)):
                key = (d, s, h)
                if key not in self.ids:
                    continue
                zz = z + 4 - s if d == "+" else z - 4 + s
                value = self.own(zz, h)
                if (d, s - 1, h) in self.ids:
                    value = value + self.got((d, s - 1, h))
                self.put(key, value, d_zp if d == "+" else d_zm)

        def close(self):
            for h in (0, 1):
                tot[h * PW:(h + 1) * PW, :] = (
                    self.own(z, h) + self.got(("+", 3, h)) + self.got(("-", 3, h))
                )
            self.put(("x", 0, 0), tot[pl.ds(pl.multiple_of((1 - xl) * PW, PW), PW), :], d_xl)

        def result(self):
            return tot[pl.ds(pl.multiple_of(xl * PW, PW), PW), :] + self.got(("x", 0, 0))

    product(acc, po, cv)
    store_cov = pltpu.make_async_copy(cv, cov_hbm, load_sem.at[6])
    store_cov.start()
    rs2 = Scatter(acc, st2, rv2)
    rs1 = Scatter(p1, st1, rv1)
    rs2.step(0)
    gc.s1()
    rs2.step(1)
    gc.s2()
    rs2.step(2)
    gc.s3()
    rs2.step(3)
    gc.s4()
    rs2.close()
    gc.s5()

    product(p1, pc, om)
    second_sum = rs2.result()
    acc[0:PW, :] = second_sum
    rs1.step(0)
    rs1.step(1)

    omega_vals = ov[...]
    lane = lax.broadcasted_iota(jnp.int32, (PW, width), 1)
    sub = lax.broadcasted_iota(jnp.int32, (PW, width), 0)
    diagonal = (lane == sub) & (r == c)
    own_diag = jnp.where(diagonal, omega_vals, 1.0)
    terms = 0.5 * omega_vals * acc[0:PW, :] + jnp.where(
        diagonal, -jnp.log(own_diag), penalty * jnp.abs(omega_vals)
    )
    tr[...] = jnp.zeros_like(tr)
    part = terms[:, 0:128]
    for t in range(1, width // 128):
        part = part + terms[:, t * 128:(t + 1) * 128]
    tr[0:PW, :] = part
    line = jnp.sum(jnp.transpose(tr[...]), axis=0, keepdims=True)
    oslots[pl.ds(pl.multiple_of(r * 8, 8), 8), :] = jnp.broadcast_to(line, (8, 128))
    oid = new(16)

    rs1.step(2)
    mine = rows(oslots, r * 8, 8, 8)
    for i in range(1, 16):
        send(oid + i, mine, mine, (lax.rem(r + i, 16), c))
    rs1.step(3)
    rs1.close()
    for i in range(1, 16):
        arrived(oid + i, rows(oslots, lax.rem(r + 16 - i, 16) * 8, 8, 8))
    total = oslots[0:8, :]
    for i in range(1, 16):
        total = total + oslots[i * 8:(i + 1) * 8, :]
    obj_ref[...] = total / P_SIZE

    both = rs1.result() + acc[0:PW, :]
    gradient = 0.5 * both - jnp.where(diagonal, 1.0 / own_diag, 0.0)
    stepped = omega_vals - step_size * gradient
    limit = step_size * penalty
    shrunk = stepped - jnp.clip(stepped, -limit, limit)
    panel_ref[...] = jnp.where(diagonal, stepped, shrunk).astype(jnp.bfloat16)

    store_cov.wait()
    for d in started:
        d.wait_send()

    @pl.when(shift != 0)
    def _():
        for h in halves:
            to_mid(h).wait_send()

    @pl.when(jnp.logical_not(tr_local))
    def _():
        for h in halves:
            to_slot(h).wait_send()


def per_device(cell_batch, cov_prior, omega_prior):
    piece, width = cell_batch.shape
    any_ = pl.BlockSpec(memory_space=pl.ANY)
    vmem = pl.BlockSpec(memory_space=pltpu.VMEM)
    bf, f32 = jnp.bfloat16, jnp.float32
    cov, panel, obj = pl.pallas_call(
        kernel,
        out_shape=(
            jax.ShapeDtypeStruct((width, width), bf),
            jax.ShapeDtypeStruct((PW, width), bf),
            jax.ShapeDtypeStruct((8, 128), f32),
        ),
        in_specs=[any_] * 3,
        out_specs=(any_, vmem, vmem),
        scratch_shapes=[
            pltpu.VMEM((16 * piece, width), bf),
            pltpu.VMEM((16 * piece, width), bf),
            pltpu.VMEM((piece, width), bf),
            pltpu.VMEM((16 * PW, width), bf),
            pltpu.VMEM((16 * PW, width), bf),
            pltpu.VMEM((width, width), bf),
            pltpu.VMEM((width, width), bf),
            pltpu.VMEM((width, width), f32),
            pltpu.VMEM((16 * PW, width), f32),
            pltpu.VMEM((PW, width), f32),
            pltpu.VMEM((15 * PW, width), bf),
            pltpu.VMEM((15 * PW, width), bf),
            pltpu.VMEM((15 * PW, width), bf),
            pltpu.VMEM((15 * PW, width), bf),
            pltpu.VMEM((2 * PW, width), f32),
            pltpu.VMEM((128, 128), f32),
            pltpu.VMEM((128, 128), f32),
            pltpu.SemaphoreType.DMA((N_SEM,)),
            pltpu.SemaphoreType.DMA((N_SEM,)),
            pltpu.SemaphoreType.DMA((8,)),
        ],
        compiler_params=pltpu.CompilerParams(
            collective_id=0, has_side_effects=True, vmem_limit_bytes=62 * 1024 * 1024
        ),
    )(cell_batch, cov_prior, omega_prior)
    return cov, panel, obj[0, :PW]


def solution(mesh):
    return jax.shard_map(
        per_device,
        mesh=mesh,
        in_specs=(P("col", "row"), P("row", "col"), P("row", "col")),
        out_specs=(P("row", "col"), P("col", "row"), P("col")),
        check_vma=False,
    )
```

```python
import functools

import jax
import jax.numpy as jnp
from jax import lax
from jax.experimental import pallas as pl
from jax.experimental.pallas import tpu as pltpu
from jax.sharding import PartitionSpec as P

P_SIZE = 20480
PW = 64

decay_weight = 0.5
step_size = 0.2
penalty = 1.0

MESH = pl.DeviceIdType.MESH
N_SEM = 192
XROWS = 64


def rows(ref, start, size, unit=16):
    if isinstance(start, int):
        return ref.at[pl.ds(start, size), :]
    return ref.at[pl.ds(pl.multiple_of(start, unit), size), :]


def nt(a, b):
    return lax.dot_general(a, b, (((1,), (1,)), ((), ())), preferred_element_type=jnp.float32)


def kernel(
    x_hbm, s_hbm, om_hbm, cov_hbm, panel_ref, obj_ref,
    xr, xc, mid, po, pc, om, cv, acc, p1, ov, st2, rv2, st1, rv1, tot, oslots, tr,
    send_sem, recv_sem, load_sem,
):
    r = lax.axis_index("row")
    c = lax.axis_index("col")
    y, xh, core = lax.div(r, 4), lax.rem(lax.div(r, 2), 2), lax.rem(r, 2)
    z, xl = lax.div(c, 2), lax.rem(c, 2)
    width = om.shape[0]
    piece = x_hbm.shape[0]

    def rowid(yy, hh, kk):
        return lax.rem(yy + 8, 4) * 4 + hh * 2 + kk

    def colid(zz, ll):
        return lax.rem(zz + 16, 8) * 2 + ll

    d_zp, d_zm = (r, colid(z + 1, xl)), (r, colid(z - 1, xl))
    d_xl = (r, colid(z, 1 - xl))
    d_yp, d_ym = (rowid(y + 1, xh, core), c), (rowid(y - 1, xh, core), c)
    d_xh = (rowid(y, 1 - xh, core), c)
    d_core = (rowid(y, xh, 1 - core), c)

    shift = lax.rem(lax.div(z + xh, 2), 4)
    d_mid = (rowid(y + shift, xh, core), c)
    from_row = rowid(y + 4 - shift, xh, core)
    to_row = lax.rem(c + from_row - core, 16)
    d_tr = (to_row, from_row)
    tr_local = (to_row == r) & (from_row == c)
    cells = lax.rem(r + 16 - 2 * z, 16)
    back = lax.rem(lax.div(lax.div(cells, 2) + lax.rem(z, 2), 2), 4)
    d_src = (rowid(lax.div(z, 2) + back, lax.rem(z, 2), xl), cells)

    load_x = pltpu.make_async_copy(x_hbm, rows(xr, c * piece, piece), load_sem.at[0])
    load_x.start()
    load_po = pltpu.make_async_copy(om_hbm.at[pl.ds(0, PW), :], rows(po, r * PW, PW), load_sem.at[1])
    load_po.start()
    load_om = pltpu.make_async_copy(om_hbm, om, load_sem.at[2])
    load_om.start()
    load_s = pltpu.make_async_copy(s_hbm, cv, load_sem.at[3])
    load_s.start()

    barrier = pltpu.get_barrier_semaphore()

    def greet(dev):
        pl.semaphore_signal(barrier, inc=1, device_id=dev, device_id_type=MESH)

    for i in range(1, 16):
        greet((lax.rem(r + i, 16), c))
    for dev in (d_zp, d_zm, d_xl):
        greet(dev)

    @pl.when(jnp.logical_not(tr_local))
    def _():
        greet(d_src)
        pl.semaphore_wait(barrier, 19)

    @pl.when(tr_local)
    def _():
        pl.semaphore_wait(barrier, 18)

    started = []
    count = [0]

    def new(n=1):
        first = count[0]
        count[0] += n
        assert count[0] <= N_SEM
        return first

    def desc(i, src, dst, dev):
        return pltpu.make_async_remote_copy(
            src_ref=src, dst_ref=dst, send_sem=send_sem.at[i], recv_sem=recv_sem.at[i],
            device_id=dev, device_id_type=MESH,
        )

    def send(i, src, dst, dev):
        d = desc(i, src, dst, dev)
        d.start()
        started.append(d)

    def arrived(i, slot):
        desc(i, slot, slot, d_core).wait_recv()

    class RowGather:
        def __init__(self, buf, m):
            self.buf, self.m, self.b = buf, m, new(19)
            self.h = m // 2

        def slot(self, yy, hh, kk, lo=0, n=None):
            return rows(self.buf, rowid(yy, hh, kk) * self.m + lo, n or self.m)

        def go(self, i, dev, yy, hh, lo=0, n=None):
            s = self.slot(yy, hh, core, lo, n)
            send(self.b + i, s, s, dev)

        def wait(self, i, yy, hh, lo=0, n=None, kk=None):
            arrived(self.b + i, self.slot(yy, hh, core if kk is None else kk, lo, n))

        def s0(self):
            self.go(0, d_xh, y, xh)
            self.go(1, d_yp, y, xh)
            self.go(2, d_ym, y, xh)
            self.go(9, d_core, y, xh)

        def s1(self):
            o = 1 - xh
            self.wait(0, y, o)
            self.go(3, d_yp, y, o)
            self.go(4, d_ym, y, o)
            self.go(10, d_core, y, o)

        def s2(self):
            h = self.h
            self.wait(1, y - 1, xh)
            self.go(5, d_yp, y - 1, xh, h, h)
            self.wait(2, y + 1, xh)
            self.go(6, d_ym, y + 1, xh, 0, h)
            self.go(11, d_core, y - 1, xh)
            self.go(12, d_core, y + 1, xh)

        def s3(self):
            h, o = self.h, 1 - xh
            self.wait(3, y - 1, o)
            self.go(7, d_yp, y - 1, o, h, h)
            self.wait(4, y + 1, o)
            self.go(8, d_ym, y + 1, o, 0, h)
            self.go(13, d_core, y - 1, o)
            self.go(14, d_core, y + 1, o)

        def s4(self):
            h, o = self.h, 1 - xh
            self.wait(5, y + 2, xh, h, h)
            self.go(15, d_core, y + 2, xh, h, h)
            self.wait(6, y + 2, xh, 0, h)
            self.go(16, d_core, y + 2, xh, 0, h)
            self.wait(7, y + 2, o, h, h)
            self.go(17, d_core, y + 2, o, h, h)
            self.wait(8, y + 2, o, 0, h)
            self.go(18, d_core, y + 2, o, 0, h)

        def s5(self):
            h, o, k = self.h, 1 - xh, 1 - core
            self.wait(9, y, xh, kk=k)
            self.wait(10, y, o, kk=k)
            self.wait(11, y - 1, xh, kk=k)
            self.wait(12, y + 1, xh, kk=k)
            self.wait(13, y - 1, o, kk=k)
            self.wait(14, y + 1, o, kk=k)
            self.wait(15, y + 2, xh, h, h, kk=k)
            self.wait(16, y + 2, xh, 0, h, kk=k)
            self.wait(17, y + 2, o, h, h, kk=k)
            self.wait(18, y + 2, o, 0, h, kk=k)

    g, gh = XROWS, XROWS // 2
    ph = piece // 2
    cg = {}

    def cid(*key):
        if key not in cg:
            cg[key] = new()
        return cg[key]

    def xs(zz, ll, lo=0, n=piece):
        return rows(xr, colid(zz, ll) * piece + lo, n)

    def csend(key, dev, zz, ll, lo=0, n=piece):
        s = xs(zz, ll, lo, n)
        send(cid(*key), s, s, dev)

    def cwait(key, zz, ll, lo=0, n=piece):
        arrived(cid(*key), xs(zz, ll, lo, n))

    rest = piece - g

    def col0():
        csend(("a",), d_xl, z, xl, 0, g)
        csend(("p+", 1), d_zp, z, xl)
        csend(("p-", 1), d_zm, z, xl)
        csend(("f", 0), d_xl, z, xl, g, rest)

    def col1():
        cwait(("a",), z, 1 - xl, 0, g)
        csend(("q+", 1), d_zp, z, 1 - xl, 0, g)
        csend(("q-", 1), d_zm, z, 1 - xl, 0, g)

    def colp(d):
        cwait(("p+", d), z - d, xl)
        if d < 3:
            csend(("p+", d + 1), d_zp, z - d, xl)
        else:
            csend(("p+", 4), d_zp, z - d, xl, 0, ph)
        csend(("f+", d), d_xl, z - d, xl, g, rest)
        cwait(("p-", d), z + d, xl)
        if d < 3:
            csend(("p-", d + 1), d_zm, z + d, xl)
        else:
            csend(("p-", 4), d_zm, z + d, xl, ph, ph)
        csend(("f-", d), d_xl, z + d, xl, g, rest)

    def colq(d):
        cwait(("q+", d), z - d, 1 - xl, 0, g)
        if d < 3:
            csend(("q+", d + 1), d_zp, z - d, 1 - xl, 0, g)
        else:
            csend(("q+", 4), d_zp, z - d, 1 - xl, 0, gh)
        cwait(("q-", d), z + d, 1 - xl, 0, g)
        if d < 3:
            csend(("q-", d + 1), d_zm, z + d, 1 - xl, 0, g)
        else:
            csend(("q-", 4), d_zm, z + d, 1 - xl, gh, gh)

    def colp4():
        cwait(("p-", 4), z + 4, xl, ph, ph)
        csend(("f", 4), d_xl, z + 4, xl, ph, ph)
        cwait(("p+", 4), z + 4, xl, 0, ph)

    def colq4():
        cwait(("q+", 4), z + 4, 1 - xl, 0, gh)
        cwait(("q-", 4), z + 4, 1 - xl, gh, gh)

    def colf(d):
        if d == 0:
            cwait(("f", 0), z, 1 - xl, g, rest)
        elif d == 4:
            cwait(("f", 4), z + 4, 1 - xl, ph, ph)
        else:
            cwait(("f+", d), z - d, 1 - xl, g, rest)
            cwait(("f-", d), z + d, 1 - xl, g, rest)

    assert g == ph

    gx = RowGather(xc, piece)
    go_ = RowGather(po, PW)
    tid = new(4)
    halves = (0, 1)
    load_x.wait()

    def to_mid(h):
        return desc(tid + h, rows(xr, c * piece + h * ph, ph), rows(mid, h * ph, ph), d_mid)

    def to_slot(h):
        return desc(tid + 2 + h, rows(mid, h * ph, ph), rows(xc, to_row * piece + h * ph, ph), d_tr)

    def keep():
        return pltpu.make_async_copy(rows(xr, c * piece, piece), mid, load_sem.at[4])

    def land():
        return pltpu.make_async_copy(mid, rows(xc, r * piece, piece), load_sem.at[7])

    @pl.when(shift != 0)
    def _():
        for h in halves:
            to_mid(h).start()

    @pl.when(shift == 0)
    def _():
        keep().start()

    col0()
    load_po.wait()
    go_.s0()

    @pl.when(shift == 0)
    def _():
        keep().wait()

    for h in halves:
        @pl.when(shift != 0)
        def _(h=h):
            to_mid(h).wait_recv()

        @pl.when(jnp.logical_not(tr_local))
        def _(h=h):
            to_slot(h).start()

    @pl.when(tr_local)
    def _():
        land().start()

    acc[...] = jnp.zeros_like(acc)
    col1()
    go_.s1()
    colp(1)
    colq(1)
    go_.s2()

    @pl.when(jnp.logical_not(tr_local))
    def _():
        for h in halves:
            desc(tid + 2 + h, rows(mid, h * ph, ph), rows(xc, r * piece + h * ph, ph), d_tr).wait_recv()

    @pl.when(tr_local)
    def _():
        land().wait()

    gx.s0()
    go_.s3()
    gx.s1()
    colp(2)
    gx.s2()
    go_.s4()
    colq(2)
    gx.s3()
    load_om.wait()
    turned = jnp.transpose(om[:, :128].astype(jnp.float32))
    ov[...] = turned[:PW, :]
    colp(3)
    gx.s4()
    colq(3)
    gx.s5()

    tile = 256

    def accumulate(lo, n):
        def body(i, carry):
            j = lax.rem(z + lo + i + 8, 8)
            k0 = pl.multiple_of(j * 2 * piece, 2 * piece)
            s0 = pl.multiple_of(lax.rem(j + z, 8) * 2 * piece, 2 * piece)

            def inner(m, carry2):
                m0 = pl.multiple_of(m * tile, tile)
                a = xr[pl.ds(k0, 2 * piece), pl.ds(m0, tile)]
                b = xc[pl.ds(s0, 2 * piece), :]
                acc[pl.ds(m0, tile), :] += lax.dot_general(
                    a, b, (((0,), (0,)), ((), ())), preferred_element_type=jnp.float32
                )
                return carry2

            return lax.fori_loop(0, width // tile, inner, carry)

        lax.fori_loop(0, n, body, 0)

    colf(0)
    colf(1)
    colf(2)
    accumulate(-2, 5)
    colp4()
    colf(3)
    accumulate(3, 1)
    accumulate(-3, 1)
    colq4()
    colf(4)
    accumulate(4, 1)
    go_.s5()

    scale_new = (1.0 - decay_weight) / 2048
    load_s.wait()

    def finalize(lo, n):
        lo = lo if isinstance(lo, int) else pl.multiple_of(lo, 128)
        prior = cv[pl.ds(lo, n), :].astype(jnp.float32)
        cv[pl.ds(lo, n), :] = (decay_weight * prior + scale_new * acc[pl.ds(lo, n), :]).astype(jnp.bfloat16)

    finalize(0, 128)
    own_cov = pltpu.make_async_copy(cv.at[pl.ds(0, PW), :], rows(pc, r * PW, PW), load_sem.at[5])

    def fin_body(i, carry):
        finalize(128 + i * 128, 128)
        return carry

    lax.fori_loop(0, 2, fin_body, 0)
    own_cov.start()
    own_cov.wait()
    gc = RowGather(pc, PW)
    gc.s0()
    lax.fori_loop(2, width // 128 - 1, fin_body, 0)

    def product(dst, left, right, d):
        def body(i, carry):
            zz = lax.rem(z + 8 + d * (1 - 2 * i), 8)
            m0 = pl.multiple_of(zz * 2 * PW, 2 * PW)
            dst[pl.ds(m0, 2 * PW), :] = nt(left[pl.ds(m0, 2 * PW), :], right[...])
            return carry

        lax.fori_loop(0, 1 if d in (0, 4) else 2, body, 0)

    class Scatter:
        def __init__(self, src, st, rv):
            self.src, self.st, self.rv = src, st, rv
            self.ids = {}
            for n, key in enumerate(
                [("+", 0, 0), ("-", 0, 1)]
                + [(d, s, h) for s in (1, 2, 3) for d in "+-" for h in (0, 1)]
                + [("x", 0, 0)]
            ):
                self.ids[key] = (n, new())

        def own(self, zz, h):
            return self.src[pl.ds(pl.multiple_of(colid(zz, h) * PW, PW), PW), :]

        def slot(self, buf, key):
            n = self.ids[key][0]
            return buf.at[pl.ds(n * PW, PW), :]

        def got(self, key):
            s = self.slot(self.rv, key)
            arrived(self.ids[key][1], s)
            return s[...].astype(jnp.float32)

        def put(self, key, value, dev):
            s = self.slot(self.st, key)
            s[...] = value.astype(jnp.bfloat16)
            send(self.ids[key][1], s, self.slot(self.rv, key), dev)

        def step(self, s):
            for d, h in ((("+"), 0), ("-", 1), ("-", 0), ("+", 1)):
                key = (d, s, h)
                if key not in self.ids:
                    continue
                zz = z + 4 - s if d == "+" else z - 4 + s
                value = self.own(zz, h)
                if (d, s - 1, h) in self.ids:
                    value = value + self.got((d, s - 1, h))
                self.put(key, value, d_zp if d == "+" else d_zm)

        def close(self):
            for h in (0, 1):
                tot[h * PW:(h + 1) * PW, :] = (
                    self.own(z, h) + self.got(("+", 3, h)) + self.got(("-", 3, h))
                )
            self.put(("x", 0, 0), tot[pl.ds(pl.multiple_of((1 - xl) * PW, PW), PW), :], d_xl)

        def result(self):
            return tot[pl.ds(pl.multiple_of(xl * PW, PW), PW), :] + self.got(("x", 0, 0))

    store_cov = pltpu.make_async_copy(cv, cov_hbm, load_sem.at[6])
    store_cov.start()
    rs2 = Scatter(acc, st2, rv2)
    rs1 = Scatter(p1, st1, rv1)
    product(acc, po, cv, 4)
    rs2.step(0)
    product(acc, po, cv, 3)
    gc.s1()
    rs2.step(1)
    product(acc, po, cv, 2)
    gc.s2()
    rs2.step(2)
    gc.s3()
    product(acc, po, cv, 1)
    rs2.step(3)
    gc.s4()
    product(acc, po, cv, 0)
    rs2.close()
    gc.s5()

    product(p1, pc, om, 4)
    rs1.step(0)
    product(p1, pc, om, 3)
    rs1.step(1)
    second_sum = rs2.result()
    acc[0:PW, :] = second_sum

    omega_vals = ov[...]
    lane = lax.broadcasted_iota(jnp.int32, (PW, width), 1)
    sub = lax.broadcasted_iota(jnp.int32, (PW, width), 0)
    diagonal = (lane == sub) & (r == c)
    own_diag = jnp.where(diagonal, omega_vals, 1.0)
    terms = 0.5 * omega_vals * acc[0:PW, :] + jnp.where(
        diagonal, -jnp.log(own_diag), penalty * jnp.abs(omega_vals)
    )
    tr[...] = jnp.zeros_like(tr)
    part = terms[:, 0:128]
    for t in range(1, width // 128):
        part = part + terms[:, t * 128:(t + 1) * 128]
    tr[0:PW, :] = part
    line = jnp.sum(jnp.transpose(tr[...]), axis=0, keepdims=True)
    oslots[pl.ds(pl.multiple_of(r * 8, 8), 8), :] = jnp.broadcast_to(line, (8, 128))
    oid = new(16)

    product(p1, pc, om, 2)
    rs1.step(2)
    mine = rows(oslots, r * 8, 8, 8)
    for i in range(1, 16):
        send(oid + i, mine, mine, (lax.rem(r + i, 16), c))
    product(p1, pc, om, 1)
    rs1.step(3)
    product(p1, pc, om, 0)
    rs1.close()
    for i in range(1, 16):
        arrived(oid + i, rows(oslots, lax.rem(r + 16 - i, 16) * 8, 8, 8))
    total = oslots[0:8, :]
    for i in range(1, 16):
        total = total + oslots[i * 8:(i + 1) * 8, :]
    obj_ref[...] = total / P_SIZE

    both = rs1.result() + acc[0:PW, :]
    gradient = 0.5 * both - jnp.where(diagonal, 1.0 / own_diag, 0.0)
    stepped = omega_vals - step_size * gradient
    limit = step_size * penalty
    shrunk = stepped - jnp.clip(stepped, -limit, limit)
    panel_ref[...] = jnp.where(diagonal, stepped, shrunk).astype(jnp.bfloat16)

    store_cov.wait()
    for d in started:
        d.wait_send()

    @pl.when(shift != 0)
    def _():
        for h in halves:
            to_mid(h).wait_send()

    @pl.when(jnp.logical_not(tr_local))
    def _():
        for h in halves:
            to_slot(h).wait_send()


def per_device(cell_batch, cov_prior, omega_prior):
    piece, width = cell_batch.shape
    any_ = pl.BlockSpec(memory_space=pl.ANY)
    vmem = pl.BlockSpec(memory_space=pltpu.VMEM)
    bf, f32 = jnp.bfloat16, jnp.float32
    cov, panel, obj = pl.pallas_call(
        kernel,
        out_shape=(
            jax.ShapeDtypeStruct((width, width), bf),
            jax.ShapeDtypeStruct((PW, width), bf),
            jax.ShapeDtypeStruct((8, 128), f32),
        ),
        in_specs=[any_] * 3,
        out_specs=(any_, vmem, vmem),
        scratch_shapes=[
            pltpu.VMEM((16 * piece, width), bf),
            pltpu.VMEM((16 * piece, width), bf),
            pltpu.VMEM((piece, width), bf),
            pltpu.VMEM((16 * PW, width), bf),
            pltpu.VMEM((16 * PW, width), bf),
            pltpu.VMEM((width, width), bf),
            pltpu.VMEM((width, width), bf),
            pltpu.VMEM((width, width), f32),
            pltpu.VMEM((16 * PW, width), f32),
            pltpu.VMEM((PW, width), f32),
            pltpu.VMEM((15 * PW, width), bf),
            pltpu.VMEM((15 * PW, width), bf),
            pltpu.VMEM((15 * PW, width), bf),
            pltpu.VMEM((15 * PW, width), bf),
            pltpu.VMEM((2 * PW, width), f32),
            pltpu.VMEM((128, 128), f32),
            pltpu.VMEM((128, 128), f32),
            pltpu.SemaphoreType.DMA((N_SEM,)),
            pltpu.SemaphoreType.DMA((N_SEM,)),
            pltpu.SemaphoreType.DMA((8,)),
        ],
        compiler_params=pltpu.CompilerParams(
            collective_id=0, has_side_effects=True, vmem_limit_bytes=62 * 1024 * 1024
        ),
    )(cell_batch, cov_prior, omega_prior)
    return cov, panel, obj[0, :PW]


def solution(mesh):
    return jax.shard_map(
        per_device,
        mesh=mesh,
        in_specs=(P("col", "row"), P("row", "col"), P("row", "col")),
        out_specs=(P("row", "col"), P("col", "row"), P("col")),
        check_vma=False,
    )
```
